512 devices in a mesh: group: 64 (over y_lo, z, core), tensor: 8 (over y_hi, x).
Axes of the slice: x: 4, y: 8 (y_hi: 2, y_lo: 4; y = y_hi * 4 + y_lo), z: 8, core: 2. Of those that a mesh axis runs over, the one named last changes fastest.
Arguments:
- turns: bfloat16 [64, 1024, 4096], P('group', 'tensor'), may hold values from -16 to 16
- query_store: bfloat16 [64, 64, 4096], P('group', None, 'tensor'), may hold values from -0.09375 to 0.09375
- key_block_holder: bfloat16 [64, 64, 4, 128], P('group'), may hold values from -0.09375 to 0.09375
- value_block_holder: bfloat16 [64, 64, 4, 128], P('group'), may hold values from -0.09375 to 0.09375
- query_bias: float32 [4096], P('tensor'), may hold values from -3 to 3
- key_projection_bias: float32 [512], replicated, may hold values from -3 to 3
- value_projection_bias: float32 [512], replicated, may hold values from -3 to 3
- owner: int32 [64], replicated, may hold values from 0 to 63, each once
- lengths: int32 [64], P('group'), may hold values from 1 to 1024, as said below
Outputs:
- attended: bfloat16 [64, 1024, 4096], P('group', None, 'tensor')
The draws below stay inside these ranges and needn't reach their ends.
Inputs may be any that keep to these rules, and one draw needn't show every extreme that they name: `owner`: each group index holds exactly one block. `lengths`: some group's turn fills all 1024 positions.
All inputs are finite; a program needn't handle non-finite values.
Results may differ from the reference program's by a relative error of at most 0.0055.
The reference program's roundings to bfloat16 on the way (of `weights`) count: a program that leaves them out, or rounds other values in their place, can miss the bound.
Values may be sent and summed in bfloat16 or wider, within the bound.
No kernel may reach another device: no remote copies, remote signals or barrier semaphores. Data moves between devices by JAX's collectives and lax.ppermute only.
A program may use at most 128 MiB of HBM per device.

```python
import jax
import jax.numpy as jnp
from jax import lax

INPUT_FEATURES = 4096
QUERY_HEADS = 32
KEY_VALUE_HEADS = 4
HEAD_SIZE = 128
ROLLOUT_GROUPS = 64
TURN_TOKENS = 1024
OWNED_BLOCK_ROWS = 64


def draw_turns(key, part):
    return jnp.clip(jax.random.normal(key, (ROLLOUT_GROUPS, TURN_TOKENS, INPUT_FEATURES), jnp.float32), -4.0, 4.0).astype(jnp.bfloat16)


def draw_lengths(key, part):
    first, second = jax.random.split(jax.random.fold_in(key, 7))
    values = jax.random.randint(first, (ROLLOUT_GROUPS,), 1, TURN_TOKENS + 1)
    full_at = jax.random.randint(second, (), 0, ROLLOUT_GROUPS)
    return values.at[full_at].set(TURN_TOKENS).astype(jnp.int32)


def shard_levels(stream_key, shape, shards, low, top_value):
    level, own = 1.0, jax.random.fold_in(stream_key, 6)
    for axis_at, blocks in shards:
        heights = jnp.exp(jax.random.uniform(jax.random.fold_in(own, axis_at), (blocks,), jnp.float32, low / len(shards), top_value / len(shards)))
        level = level * jnp.repeat(heights, shape[axis_at] // blocks).reshape([-1 if axis == axis_at else 1 for axis in range(len(shape))])
    return level


def scatter_about(own_key, extent, width, limit, pieces=(), kind=jnp.bfloat16):
    entries = width * jax.random.normal(own_key, extent, jnp.float32)
    if pieces:
        entries = entries * shard_levels(own_key, extent, pieces, -0.22, 0.18)
    return jnp.clip(entries, -limit, limit).astype(kind)


def setup_inputs(seed: int = 0) -> dict:
    key_list = jax.random.split(jax.random.key(seed), 10)
    turns = draw_turns(jax.random.fold_in(key_list[9], 71), 0)
    query_store = scatter_about(key_list[1], (ROLLOUT_GROUPS, OWNED_BLOCK_ROWS, QUERY_HEADS * HEAD_SIZE), INPUT_FEATURES ** -0.5, 0.09375, ((0, 64), (2, 8)))
    key_block_holder = scatter_about(key_list[2], (ROLLOUT_GROUPS, OWNED_BLOCK_ROWS, KEY_VALUE_HEADS, HEAD_SIZE), INPUT_FEATURES ** -0.5, 0.09375, ((0, 64),))
    value_block_holder = scatter_about(key_list[3], (ROLLOUT_GROUPS, OWNED_BLOCK_ROWS, KEY_VALUE_HEADS, HEAD_SIZE), INPUT_FEATURES ** -0.5, 0.09375, ((0, 64),))
    query_bias = scatter_about(key_list[4], (QUERY_HEADS * HEAD_SIZE,), 0.5, 3.0, ((0, 8),), jnp.float32)
    key_projection_bias = scatter_about(key_list[5], (KEY_VALUE_HEADS * HEAD_SIZE,), 0.5, 3.0, (), jnp.float32)
    value_projection_bias = scatter_about(key_list[6], (KEY_VALUE_HEADS * HEAD_SIZE,), 0.5, 3.0, (), jnp.float32)
    owner = jax.random.permutation(key_list[7], ROLLOUT_GROUPS).astype(jnp.int32)
    lengths = draw_lengths(jax.random.fold_in(key_list[9], 71), 0)
    return {"turns": turns, "query_store": query_store, "key_block_holder": key_block_holder, "value_block_holder": value_block_holder, "query_bias": query_bias, "key_projection_bias": key_projection_bias, "value_projection_bias": value_projection_bias, "owner": owner, "lengths": lengths}


rotary_base = 1000000.0


def rotary(heads, positions):
    half = heads.shape[-1] // 2
    expo = jnp.arange(half, dtype=jnp.float32) * 2.0 / heads.shape[-1]
    freqs = rotary_base ** (-expo)
    angles = positions[:, None] * freqs[None, :]
    cosine = jnp.cos(angles)[None]
    sine = jnp.sin(angles)[None]
    first = heads[..., :half]
    second = heads[..., half:]
    return jnp.concatenate([first * cosine - second * sine, second * cosine + first * sine], axis=-1)


def reference(turns, query_store, key_block_holder, value_block_holder, query_bias, key_projection_bias, value_projection_bias, owner, lengths):
    w_query = query_store[owner].reshape(INPUT_FEATURES, QUERY_HEADS * HEAD_SIZE)
    key_weight_matrix = key_block_holder[owner].reshape(INPUT_FEATURES, KEY_VALUE_HEADS * HEAD_SIZE)
    value_weight_matrix = value_block_holder[owner].reshape(INPUT_FEATURES, KEY_VALUE_HEADS * HEAD_SIZE)
    query_per_key_head = QUERY_HEADS // KEY_VALUE_HEADS
    positions = jnp.arange(TURN_TOKENS, dtype=jnp.float32)
    index = jnp.arange(TURN_TOKENS, dtype=jnp.int32)
    causal = index[None, :] <= index[:, None]

    def one_group(inputs):
        hidden, length = inputs
        raw_query = jnp.dot(hidden, w_query, preferred_element_type=jnp.float32) + query_bias
        unbiased_key = jnp.dot(hidden, key_weight_matrix, preferred_element_type=jnp.float32) + key_projection_bias
        unbiased_value = jnp.dot(hidden, value_weight_matrix, preferred_element_type=jnp.float32) + value_projection_bias
        raw_query = raw_query.reshape(TURN_TOKENS, QUERY_HEADS, HEAD_SIZE).transpose(1, 0, 2)
        unbiased_key = unbiased_key.reshape(TURN_TOKENS, KEY_VALUE_HEADS, HEAD_SIZE).transpose(1, 0, 2)
        unbiased_value = unbiased_value.reshape(TURN_TOKENS, KEY_VALUE_HEADS, HEAD_SIZE).transpose(1, 0, 2)
        query = rotary(raw_query, positions).astype(jnp.bfloat16)
        key = rotary(unbiased_key, positions).astype(jnp.bfloat16)
        value = unbiased_value.astype(jnp.bfloat16)
        key_full = jnp.repeat(key, query_per_key_head, axis=0).astype(jnp.float32)
        value_full = jnp.repeat(value, query_per_key_head, axis=0).astype(jnp.float32)
        scores = jnp.einsum("htd,hsd->hts", query.astype(jnp.float32), key_full) * (HEAD_SIZE ** -0.5)
        scores = jnp.where(causal[None], scores, -jnp.inf)
        top = jnp.max(scores, axis=-1, keepdims=True)
        expd = jnp.exp(scores - top)
        weights = (expd / jnp.sum(expd, axis=-1, keepdims=True)).astype(jnp.bfloat16)
        mixed = jnp.einsum("hts,hsd->htd", weights.astype(jnp.float32), value_full)
        mixed = mixed.transpose(1, 0, 2).reshape(TURN_TOKENS, QUERY_HEADS * HEAD_SIZE)
        live = (index < length)[:, None]
        return jnp.where(live, mixed, 0.0).astype(jnp.bfloat16)

    return lax.map(one_group, (turns, lengths))
```

```python
import functools

import jax
import jax.numpy as jnp
from jax import lax
from jax.experimental import pallas as pl
from jax.experimental.pallas import tpu as pltpu
from jax.sharding import PartitionSpec as P


HEAD_SIZE = 128
FEATURES = 4096
TOKENS = 1024
GROUPS = 64
ROWS = 64
HEADS_DEV = 4
QCOLS = HEADS_DEV * HEAD_SIZE
COLS = QCOLS + 2 * HEAD_SIZE
SPAN = 256
rotary_base = 1000000.0


def group_perm(dy=0, dz=0, dc=0):
    out = []
    for g in range(64):
        y, z, c = g // 16, (g // 2) % 8, g % 2
        out.append((g, ((y + dy) % 4) * 16 + ((z + dz) % 8) * 2 + (c + dc) % 2))
    return out


def tensor_perm(dy=0, dx=0):
    return [(t, ((t // 4 + dy) % 2) * 4 + (t % 4 + dx) % 4) for t in range(8)]


def send_group(a, **k):
    return lax.ppermute(a, "group", group_perm(**k))


def send_tensor(a, **k):
    return lax.ppermute(a, "tensor", tensor_perm(**k))


def kernel(
    n_pieces,
    row_ref,
    pos_ref,
    len_ref,
    *refs,
):
    pieces = refs[:n_pieces]
    w_mine, w_other, bias_ref, cos_ref, sin_ref, out_ref = refs[n_pieces : n_pieces + 6]
    x_buf, w_buf, q_buf, k_buf, v_buf, x_sem, w_sem = refs[n_pieces + 6 :]

    def fetch(b, carry):
        p = pos_ref[b]
        dst = w_buf.at[pl.ds(pl.multiple_of(b * ROWS, ROWS), ROWS), :]

        @pl.when(p < 32)
        def _():
            pltpu.make_async_copy(w_mine.at[p], dst, w_sem).start()

        @pl.when(p >= 32)
        def _():
            pltpu.make_async_copy(w_other.at[p - 32], dst, w_sem).start()

        return carry

    lax.fori_loop(0, GROUPS, fetch, 0)
    for i, piece in enumerate(pieces):
        first = pl.multiple_of(row_ref[i], 32)
        pltpu.make_async_copy(piece, x_buf.at[pl.ds(first, piece.shape[0]), :], x_sem).start()
    pltpu.make_async_copy(w_buf, w_buf, w_sem).wait()
    pltpu.make_async_copy(x_buf, x_buf, x_sem).wait()

    def project(i, carry):
        rows = pl.ds(pl.multiple_of(i * SPAN, SPAN), SPAN)
        acc = jnp.dot(x_buf[rows, :], w_buf[...], preferred_element_type=jnp.float32)
        acc = acc + bias_ref[...]
        cos, sin = cos_ref[rows, :], sin_ref[rows, :]
        for h in range(HEADS_DEV + 1):
            a = acc[:, h * HEAD_SIZE : (h + 1) * HEAD_SIZE]
            r = (a * cos + pltpu.roll(a, HEAD_SIZE // 2, 1) * sin).astype(jnp.bfloat16)
            if h < HEADS_DEV:
                q_buf[h, rows, :] = r
            else:
                k_buf[rows, :] = r
        v_buf[rows, :] = acc[:, (HEADS_DEV + 1) * HEAD_SIZE :].astype(jnp.bfloat16)
        return carry

    lax.fori_loop(0, TOKENS // SPAN, project, 0)

    scale = HEAD_SIZE ** (-0.5)
    live_len = len_ref[0]
    for i in range(TOKENS // SPAN):
        first, last = i * SPAN, (i + 1) * SPAN
        keys = k_buf[:last, :]
        values = v_buf[:last, :]
        qpos = first + lax.broadcasted_iota(jnp.int32, (SPAN, last), 0)
        kpos = lax.broadcasted_iota(jnp.int32, (SPAN, last), 1)
        causal = kpos <= qpos
        live = first + lax.broadcasted_iota(jnp.int32, (SPAN, HEAD_SIZE), 0) < live_len

        def attend(h, carry):
            q = q_buf[h, first:last, :]
            s = lax.dot_general(
                q, keys, (((1,), (1,)), ((), ())), preferred_element_type=jnp.float32
            )
            s = jnp.where(causal, s * scale, -jnp.inf)
            top = jnp.max(s, axis=-1, keepdims=True)
            e = jnp.exp(s - top)
            w = (e * (1.0 / jnp.sum(e, axis=-1, keepdims=True))).astype(jnp.bfloat16)
            o = jnp.dot(w, values, preferred_element_type=jnp.float32)
            o = jnp.where(live, o, 0.0).astype(jnp.bfloat16)
            out_ref[first:last, pl.ds(pl.multiple_of(h * HEAD_SIZE, HEAD_SIZE), HEAD_SIZE)] = o
            return carry

        lax.fori_loop(0, HEADS_DEV, attend, 0)


def per_device(
    turns,
    query_store,
    key_block_holder,
    value_block_holder,
    query_bias,
    key_projection_bias,
    value_projection_bias,
    owner,
    lengths,
):
    t = lax.axis_index("tensor")
    g = lax.axis_index("group")
    my_y, my_z, my_c = g // 16, (g // 2) % 8, g % 2
    my_x, my_h = t % 4, t // 4
    head = t // 2

    kv = [
        lax.dynamic_slice_in_dim(b, head, 1, 2).reshape(1, ROWS, HEAD_SIZE)
        for b in (key_block_holder, value_block_holder)
    ]
    block = jnp.concatenate([query_store] + kv, axis=2)
    bias = jnp.concatenate(
        [query_bias]
        + [
            lax.dynamic_slice_in_dim(b, head * HEAD_SIZE, HEAD_SIZE, 0)
            for b in (key_projection_bias, value_projection_bias)
        ]
    ).reshape(1, COLS)

    quad = jnp.concatenate([block] + [send_group(block, dy=d) for d in (1, 2, 3)], axis=0)
    ring = {0: quad}
    up = down = quad
    for e in (1, 2, 3):
        up = send_group(up, dz=1)
        down = send_group(down, dz=-1)
        ring[e], ring[8 - e] = up, down
    ring[4] = send_group(up, dz=1)
    w_mine = jnp.concatenate([ring[e] for e in range(8)], axis=0)
    w_other = send_group(w_mine, dc=1)

    mine = turns[0]
    half = mine.shape[0] // 2
    left = send_tensor(mine, dx=1)
    right = send_tensor(mine, dx=-1)
    parts = [
        (mine, 0, 0, 0),
        (left, 0, -1, 0),
        (right, 0, 1, 0),
        (send_tensor(left[:half], dx=1), 0, 2, 0),
        (send_tensor(right[half:], dx=-1), 0, 2, half),
    ]
    for k in (0, 1):
        part = send_tensor(mine[k * half : (k + 1) * half], dy=1)
        left = send_tensor(part, dx=1)
        right = send_tensor(part, dx=-1)
        last = send_tensor((left, right)[k], dx=(1, -1)[k])
        parts += [(a, 1, dx, k * half) for a, dx in ((part, 0), (left, -1), (right, 1), (last, 2))]
    pieces = [p[0] for p in parts]
    firsts = [(((my_h + dh) % 2) * 4 + (my_x + dx) % 4) * 128 + row for _, dh, dx, row in parts]
    firsts = jnp.stack(firsts).astype(jnp.int32)

    o = owner.astype(jnp.int32)
    pos = (
        ((my_z - (o // 2) % 8) % 8) * 4 + (my_y - o // 16) % 4 + jnp.where(o % 2 == my_c, 0, 32)
    ).astype(jnp.int32)

    half_size = HEAD_SIZE // 2
    expo = jnp.arange(half_size, dtype=jnp.float32) * 2.0 / HEAD_SIZE
    freqs = rotary_base ** (-expo)
    angles = jnp.arange(TOKENS, dtype=jnp.float32)[:, None] * freqs[None, :]
    cosine, sine = jnp.cos(angles), jnp.sin(angles)
    cos = jnp.concatenate([cosine, cosine], axis=1)
    sin = jnp.concatenate([-sine, sine], axis=1)

    hbm = pl.BlockSpec(memory_space=pl.ANY)
    vmem = pl.BlockSpec(memory_space=pltpu.VMEM)
    out = pl.pallas_call(
        functools.partial(kernel, len(pieces)),
        out_shape=jax.ShapeDtypeStruct((TOKENS, QCOLS), jnp.bfloat16),
        grid_spec=pltpu.PrefetchScalarGridSpec(
            num_scalar_prefetch=3,
            grid=(),
            in_specs=[hbm] * (len(pieces) + 2) + [vmem] * 3,
            out_specs=vmem,
            scratch_shapes=[
                pltpu.VMEM((TOKENS, FEATURES), jnp.bfloat16),
                pltpu.VMEM((FEATURES, COLS), jnp.bfloat16),
                pltpu.VMEM((HEADS_DEV, TOKENS, HEAD_SIZE), jnp.bfloat16),
                pltpu.VMEM((TOKENS, HEAD_SIZE), jnp.bfloat16),
                pltpu.VMEM((TOKENS, HEAD_SIZE), jnp.bfloat16),
                pltpu.SemaphoreType.DMA(()),
                pltpu.SemaphoreType.DMA(()),
            ],
        ),
        compiler_params=pltpu.CompilerParams(vmem_limit_bytes=40 << 20),
        name="project_attend",
    )(firsts, pos, lengths.astype(jnp.int32), *pieces, w_mine, w_other, bias, cos, sin)
    return out[None]


def solution(mesh):
    in_specs = (
        P("group", "tensor", None),
        P("group", None, "tensor"),
        P("group", None, None, None),
        P("group", None, None, None),
        P("tensor"),
        P(),
        P(),
        P(),
        P("group"),
    )
    out_specs = P("group", None, "tensor")

    def step(*args):
        return per_device(*args)

    step = jax.shard_map(
        step, mesh=mesh, in_specs=in_specs, out_specs=out_specs, check_vma=False
    )
    return step
```
